256 devices in a mesh: seq: 16 (over y, z_lo, core), head: 16 (over z_hi, x).
Axes of the slice: x: 4, y: 4, z: 8 (z_hi: 4, z_lo: 2; z = z_hi * 2 + z_lo), core: 2. Of those that a mesh axis runs over, the one named last changes fastest.
Arguments:
- out_grad: bfloat16 [32768, 4096], P(('seq', 'head')), may hold values from -6 to 6
- out_weight: bfloat16 [4096, 4096], P('head'), may hold values from -0.09375 to 0.09375
- queries: bfloat16 [32768, 4096], P('seq', 'head'), may hold values from -4 to 4
- key_rows: bfloat16 [32768, 4096], P('seq', 'head'), may hold values from -4 to 4
- value_rows: bfloat16 [32768, 4096], P('seq', 'head')
- gate_out: bfloat16 [32768, 4096], P('seq', 'head'), may hold values from -6 to 6
- doc_starts: int32 [9], replicated, may hold values from 0 to 32767, as said below
Outputs:
- grad_queries: bfloat16 [32768, 4096], P('seq', 'head')
- grad_keys: bfloat16 [32768, 4096], P('seq', 'head')
- grad_values: bfloat16 [32768, 4096], P('seq', 'head')
- grad_gate: bfloat16 [32768, 4096], P('seq', 'head')
The draws below stay inside these ranges and needn't reach their ends.
Inputs may be any that keep to these rules, and one draw needn't show every extreme that they name: `doc_starts`: strictly increasing token offsets; the first is 0 and the last is 32767.
All inputs are finite; a program needn't handle non-finite values.
Results may differ from the reference program's by a relative error of at most 0.0058.
Values may be sent and summed in bfloat16 or wider, within the bound.
A program may use at most 128 MiB of HBM per device.

```python
import math
import jax
import jax.numpy as jnp
from jax import lax

D = 4096
HEADS = 32
HEAD_DIM = 128
BLK = 512
HDIM = 4096
TOKENS = 32768
DOCS = 9


def draw_value_rows(key, part):
    first_key = jax.random.fold_in(key, 11)
    second_key = jax.random.fold_in(key, 12)
    columns = jnp.arange(HDIM, dtype=jnp.int32)
    head_pos = (columns // HEAD_DIM).astype(jnp.float32) / (HEADS - 1)
    rising = jnp.exp(head_pos * math.log(3.0))
    spread = jnp.exp(jax.random.uniform(second_key, (HDIM,), jnp.float32) * math.log(10.0))
    base = jnp.clip(jax.random.normal(first_key, (TOKENS, HDIM), jnp.float32), -6.0, 6.0)
    values = 0.3 * base * rising[None, :] * spread[None, :]
    return values.astype(jnp.bfloat16)


def draw_doc_starts(key, part):
    picks = jax.random.permutation(jax.random.fold_in(key, 21), TOKENS - 2)[:DOCS - 2] + 1
    ordered = jnp.sort(picks.astype(jnp.int32))
    first = jnp.zeros((1,), jnp.int32)
    last = jnp.full((1,), TOKENS - 1, jnp.int32)
    return jnp.concatenate([first, ordered, last])


def shard_levels(stream_key, shape, cuts, smallest, high):
    gain, own = 1.0, jax.random.fold_in(stream_key, 6)
    for axis_at, shards_of in cuts:
        draws = jnp.exp(jax.random.uniform(jax.random.fold_in(own, axis_at), (shards_of,), jnp.float32, smallest / len(cuts), high / len(cuts)))
        gain = gain * jnp.repeat(draws, shape[axis_at] // shards_of).reshape([-1 if axis == axis_at else 1 for axis in range(len(shape))])
    return gain


def normal_values(key, dims, width, bound, shards=(), kind=jnp.bfloat16):
    result = jax.random.normal(key, dims, jnp.float32) * width
    if len(shards) > 0:
        result = shard_levels(key, dims, shards, -0.22, 0.18) * result
    return jnp.clip(result, min=-bound, max=bound).astype(kind)


def setup_inputs(seed: int = 0) -> dict:
    arg_keys = jax.random.split(jax.random.key(seed), 8)
    out_grad = normal_values(arg_keys[0], (TOKENS, D), 1.0, 6.0, ((0, 256),))
    out_weight = normal_values(arg_keys[1], (HDIM, D), D ** -0.5, 0.09375, ((0, 16),))
    queries = normal_values(arg_keys[2], (TOKENS, HDIM), 0.25, 4.0, ((0, 16), (1, 16)))
    key_rows = normal_values(arg_keys[3], (TOKENS, HDIM), 0.25, 4.0, ((0, 16), (1, 16)))
    value_rows = draw_value_rows(jax.random.fold_in(arg_keys[7], 71), 0)
    gate_out = normal_values(arg_keys[5], (TOKENS, HDIM), 1.0, 6.0, ((0, 16), (1, 16)))
    doc_starts = draw_doc_starts(jax.random.fold_in(arg_keys[7], 71), 0)
    return dict(out_grad=out_grad, out_weight=out_weight, queries=queries, key_rows=key_rows, value_rows=value_rows, gate_out=gate_out, doc_starts=doc_starts)


EPS = 1e-06

def block_masks(doc_block, mark_block):
    first_doc = doc_block[0]
    last_doc = doc_block[-1]
    keep_in = ((doc_block == first_doc) & (mark_block[0] == 0)).astype(jnp.float32)
    keep_out = (doc_block == last_doc).astype(jnp.float32)
    blocked = jnp.where((last_doc != first_doc) | (mark_block[0] == 1), jnp.float32(1.0), jnp.float32(0.0))
    order = jnp.arange(doc_block.shape[0], dtype=jnp.int32)
    causal = (order[None, :] <= order[:, None]) & (doc_block[None, :] == doc_block[:, None])
    return (keep_in, keep_out, blocked, causal.astype(jnp.float32))

def reference(out_grad, out_weight, queries, key_rows, value_rows, gate_out, doc_starts):
    f32 = jnp.float32
    bf16 = jnp.bfloat16
    positions = jnp.arange(TOKENS, dtype=jnp.int32)
    doc_ids = lax.optimization_barrier(jnp.sum((doc_starts[None, :] <= positions[:, None]).astype(jnp.int32), axis=1)) - 1
    marks = lax.optimization_barrier(jnp.sum((doc_starts[None, :] == positions[:, None]).astype(jnp.int32), axis=1))
    grad_mix = jnp.dot(out_grad.astype(f32), out_weight.astype(f32).T, preferred_element_type=f32)
    nblocks = TOKENS // BLK

    def split(array):
        return array.reshape(nblocks, BLK, HEADS, HEAD_DIM)
    query_blocks = split(queries)
    key_blocks = split(key_rows)
    value_blocks = split(value_rows)
    doc_blocks = doc_ids.reshape(nblocks, BLK)
    mark_blocks = marks.reshape(nblocks, BLK)

    def forward_step(state, inputs):
        query_b, key_b, value_b, doc_b, mark_b = inputs
        keep_in, keep_out, blocked, causal = block_masks(doc_b, mark_b)
        scores = jnp.einsum('thd,shd->hts', query_b.astype(f32), key_b.astype(f32))
        probs = (scores * causal[None]).astype(bf16)
        state_low = state.astype(bf16)
        intra = jnp.einsum('hts,she->the', probs.astype(f32), value_b.astype(f32))
        inter = jnp.einsum('thd,hde->the', query_b.astype(f32), state_low.astype(f32)) * keep_in[:, None, None]
        masked_keys = key_b * keep_out.astype(bf16)[:, None, None]
        element = jnp.einsum('shd,she->hde', masked_keys.astype(f32), value_b.astype(f32))
        return (element + (1.0 - blocked) * state, (intra + inter, state_low))
    zero_state = jnp.zeros((HEADS, HEAD_DIM, HEAD_DIM), f32)
    _, (attn_blocks, forward_low) = lax.scan(forward_step, zero_state, (query_blocks, key_blocks, value_blocks, doc_blocks, mark_blocks))
    attn_out = attn_blocks.reshape(TOKENS, HDIM)
    rms = jnp.sqrt(lax.optimization_barrier(jnp.sum(attn_out * attn_out, axis=1)) / HDIM + EPS)
    grad_gate = (grad_mix * attn_out / rms[:, None]).astype(bf16)
    gated = grad_mix * gate_out.astype(f32)
    cross = lax.optimization_barrier(jnp.sum(gated * attn_out, axis=1))
    grad_attn = (gated / rms[:, None] - attn_out * (cross / (HDIM * rms ** 3))[:, None]).astype(bf16)
    grad_blocks = split(grad_attn)

    def backward_step(state, inputs):
        query_b, key_b, value_b, grad_b, doc_b, mark_b, forward_b = inputs
        keep_in, keep_out, blocked, causal = block_masks(doc_b, mark_b)
        scores = jnp.einsum('thd,shd->hts', query_b.astype(f32), key_b.astype(f32))
        probs = (scores * causal[None]).astype(bf16).astype(f32)
        dscore = jnp.einsum('the,she->hts', grad_b.astype(f32), value_b.astype(f32))
        dprob = (dscore * causal[None]).astype(bf16).astype(f32)
        state_low = state.astype(bf16).astype(f32)
        forward_f = forward_b.astype(f32)
        grad_q = jnp.einsum('hts,shd->thd', dprob, key_b.astype(f32))
        grad_q = grad_q + keep_in[:, None, None] * jnp.einsum('the,hde->thd', grad_b.astype(f32), forward_f)
        grad_k = jnp.einsum('hts,thd->shd', dprob, query_b.astype(f32))
        grad_k = grad_k + keep_out[:, None, None] * jnp.einsum('she,hde->shd', value_b.astype(f32), state_low)
        grad_v = jnp.einsum('hts,the->she', probs, grad_b.astype(f32))
        grad_v = grad_v + keep_out[:, None, None] * jnp.einsum('shd,hde->she', key_b.astype(f32), state_low)
        masked_queries = query_b * keep_in.astype(bf16)[:, None, None]
        element = jnp.einsum('thd,the->hde', masked_queries.astype(f32), grad_b.astype(f32))
        outputs = (grad_q.astype(bf16), grad_k.astype(bf16), grad_v.astype(bf16))
        return (element + (1.0 - blocked) * state, outputs)
    _, (grad_q_blocks, grad_k_blocks, grad_v_blocks) = lax.scan(backward_step, zero_state, (query_blocks, key_blocks, value_blocks, grad_blocks, doc_blocks, mark_blocks, forward_low), reverse=True)
    return (grad_q_blocks.reshape(TOKENS, HDIM), grad_k_blocks.reshape(TOKENS, HDIM), grad_v_blocks.reshape(TOKENS, HDIM), grad_gate)
```

```python
import functools

import jax
import jax.numpy as jnp
from jax import lax
from jax.experimental import pallas as pl
from jax.experimental.pallas import tpu as pltpu
from jax.sharding import PartitionSpec as P

HD = 128
BLK = 512
HDIM = 4096
D = 4096
DOCS = 9
LEN = 2048
WID = 256
NB = 4
EPS = 1e-06
MESH = pl.DeviceIdType.MESH
f32 = jnp.float32
bf16 = jnp.bfloat16
i32 = jnp.int32

ROW0, WGT0, WY0, MIX0, FST0, RST0, SQ0, CR0, NSEM = 0, 6, 9, 33, 45, 54, 63, 78, 93


def nt(a, b):
    return lax.dot_general(a, b, (((1,), (1,)), ((), ())), preferred_element_type=f32)


def nn(a, b):
    return lax.dot_general(a, b, (((1,), (0,)), ((), ())), preferred_element_type=f32)


def tn(a, b):
    return lax.dot_general(a, b, (((0,), (0,)), ((), ())), preferred_element_type=f32)


def kernel(ds, og, w, q_h, k_h, v_h, gate_h, gq_o, gk_o, gv_o, gg_o,
           R, W, q, k, v, gate, attn, GM, SG, g, GK, GV, DC, DR, E, F, PS,
           tSs, tRs, cSs, cRs, sSs, sRs, st, sqS, sqR, crS, crR, acc, cols,
           ssem, rsem, lsem):
    s = lax.axis_index("seq")
    h = lax.axis_index("head")
    c = lax.rem(s, 2)
    zl = lax.rem(lax.div(s, 2), 2)
    y = lax.div(s, 4)
    x = lax.rem(h, 4)
    zh = lax.div(h, 4)
    n = y * 2 + zl
    d = 2 * zl - 1

    def m4(a):
        return lax.rem(a + 8, 4)

    def dev(y_, zl_, c_, zh_, x_):
        return ((y_ * 2 + zl_) * 2 + c_, zh_ * 4 + x_)

    right = dev(y, zl, c, zh, m4(x + 1))
    left = dev(y, zl, c, zh, m4(x - 1))
    up = dev(m4(y + 1), zl, c, zh, x)
    down = dev(m4(y - 1), zl, c, zh, x)
    inner = dev(y, 1 - zl, c, zh, x)
    outer = dev(y, 1 - zl, c, m4(zh + d), x)
    mate = dev(y, zl, 1 - c, zh, x)
    zh_of = (zh, m4(zh + d), m4(zh - d), m4(zh + 2))
    x_of = (x, m4(x - 1), m4(x + 1), m4(x + 2))
    y_dn, y_up, y_op = m4(y - 1), m4(y + 1), m4(y + 2)

    def rc(i, src, dst, to):
        return pltpu.make_async_remote_copy(src_ref=src, dst_ref=dst, send_sem=ssem.at[i], recv_sem=rsem.at[i],
                                            device_id=to, device_id_type=MESH)

    def head_peer(o):
        return (s, lax.rem(h + o, 16))

    def chip_peer(o):
        m = lax.rem(n + o, 8)
        return (m * 2 + c, h)

    rows = [
        rc(0, og.at[0], R.at[1, 0], right),
        rc(1, og.at[1], R.at[1, 1], right),
        rc(2, og.at[1], R.at[2, 1], left),
        rc(3, og.at[0], R.at[2, 0], left),
        rc(4, R.at[1, 0], R.at[3, 0], right),
        rc(5, R.at[2, 1], R.at[3, 1], left),
    ]
    wgt = [
        rc(WGT0, w.at[c, y], W.at[1, c, y], outer),
        rc(WGT0 + 1, W.at[1, c, y], W.at[2, c, y], inner),
        rc(WGT0 + 2, W.at[2, c, y], W.at[3, c, y], outer),
    ]
    top, bot = pl.ds(0, 16), pl.ds(16, 16)

    def wy(p):
        b = WY0 + 8 * (p - 1)
        return [
            rc(b, W.at[p, c, y], W.at[p, c, y], up),
            rc(b + 1, W.at[p, c, y], W.at[p, c, y], down),
            rc(b + 2, W.at[p, c, y], W.at[p, c, y], mate),
            rc(b + 3, W.at[p, c, y_dn, top], W.at[p, c, y_dn, top], up),
            rc(b + 4, W.at[p, c, y_up, bot], W.at[p, c, y_up, bot], down),
            rc(b + 5, W.at[p, c, y_dn], W.at[p, c, y_dn], mate),
            rc(b + 6, W.at[p, c, y_up], W.at[p, c, y_up], mate),
            rc(b + 7, W.at[p, c, y_op], W.at[p, c, y_op], mate),
        ]

    wys = {p: wy(p) for p in (1, 2, 3)}

    def mix(p, r):
        return rc(MIX0 + (p - 1) * 4 + r, SG.at[p - 1, r], GM.at[zh, x_of[r]], dev(y, zl, c, zh_of[p], x))

    local = [
        pltpu.make_async_copy(k_h, k, lsem.at[0]),
        pltpu.make_async_copy(v_h, v, lsem.at[1]),
        pltpu.make_async_copy(q_h, q, lsem.at[2]),
        pltpu.make_async_copy(gate_h, gate, lsem.at[3]),
        pltpu.make_async_copy(og, R.at[0], lsem.at[4]),
        pltpu.make_async_copy(w, W.at[0], lsem.at[5]),
    ]
    for cp in local[:3]:
        cp.start()

    barrier = pltpu.get_barrier_semaphore()
    peers = [head_peer(o) for o in range(1, 16)] + [chip_peer(o) for o in range(1, 8)] + [mate, outer]
    for to in peers:
        pl.semaphore_signal(barrier, inc=1, device_id=to, device_id_type=MESH)
    pl.semaphore_wait(barrier, len(peers))

    wgt[0].start()
    for cp in (rows[0], rows[2], rows[1], rows[3]):
        cp.start()
    for cp in local[3:]:
        cp.start()

    def cnt(t):
        total = jnp.int32(0)
        for i in range(DOCS):
            total = total + (ds[i] <= t).astype(i32)
        return total

    base = s * LEN
    edge = [cnt(base + BLK * b - 1) for b in range(NB + 1)]
    open_ = [(edge[b] == edge[b + 1]).astype(f32) for b in range(NB)]
    low, high = jnp.int32(0), jnp.int32(0)

    def edge_at(b):
        return cnt(base + BLK * b - 1)

    def rows_at(b):
        return pl.ds(pl.multiple_of(b * BLK, BLK), BLK)

    def counts(b, _):
        t = base + b * BLK + lax.broadcasted_iota(i32, (BLK, HD), 0)
        total = jnp.zeros((BLK, HD), i32)
        for i in range(DOCS):
            total = total + (t >= ds[i]).astype(i32)
        DC[rows_at(b), :] = total
        return 0

    lax.fori_loop(0, NB, counts, 0)
    t = base + lax.broadcasted_iota(i32, (8, LEN), 1)
    total = jnp.zeros((8, LEN), i32)
    for i in range(DOCS):
        total = total + (t >= ds[i]).astype(i32)
    DR[...] = total

    def wide(a):
        return jnp.concatenate([a, a], axis=1)

    def elements(b, _, left_ref, right_ref, at_end):
        r = rows_at(b)
        want = jnp.where(at_end, edge_at(b + 1), edge_at(b))
        keep = wide(DC[r, :]) == want
        a = jnp.where(keep, left_ref[r, :].astype(f32), 0.0).astype(bf16)
        both = tn(a, right_ref[r, :])
        E[b, 0] = both[:HD, :HD]
        E[b, 1] = both[HD:, HD:]
        return 0

    def exchange_send(b0, blocks):
        tS, tR = tSs.at[b0 // RST0], tRs.at[b0 // RST0]
        for hd in range(2):
            tot = jnp.zeros((HD, HD), f32)
            for b in blocks:
                tot = E[b, hd] + open_[b] * tot
            st[hd] = tot
            tS[hd] = tot.astype(bf16)
        cp = rc(b0, tS, tR, mate)
        cp.start()
        return cp

    def flag(a):
        return jnp.where(a, 1.0, 0.0).astype(f32)

    def exchange_chip(b0, cp, fwd):
        tR, cS, cR = tRs.at[b0 // RST0], cSs.at[b0 // RST0], cRs.at[b0 // RST0]
        cp.wait_recv()
        mine_open = flag(edge[0] == edge[NB])
        mate_base = (s + 1 - 2 * c) * LEN
        mate_open = flag(cnt(mate_base - 1) == cnt(mate_base + LEN - 1))
        second = (c == 1) if fwd else (c == 0)
        mine_w = jnp.where(second, jnp.float32(1.0), mate_open)
        mate_w = jnp.where(second, mine_open, jnp.float32(1.0))
        for hd in range(2):
            cS[hd] = (mine_w * st[hd] + mate_w * tR[hd].astype(f32)).astype(bf16)
        cps = [rc(b0 + o, cS.at[c], cR.at[o], chip_peer(o)) for o in range(1, 8)]
        for one in cps:
            one.start()
        return cps

    def exchange_mate(b0, cps, fwd):
        cR, sS, sR = cRs.at[b0 // RST0], sSs.at[b0 // RST0], sRs.at[b0 // RST0]
        tot = jnp.zeros((HD, HD), f32)
        for o in range(1, 8):
            cps[o - 1].wait_recv()
            src = lax.rem(n - o + 8, 8)
            if fwd:
                use = (src < n) & (cnt((src + 1) * 2 * LEN - 1) == cnt(n * 2 * LEN - 1))
            else:
                use = (src > n) & (cnt((n + 1) * 2 * LEN - 1) == cnt(src * 2 * LEN - 1))
            tot = tot + flag(use) * cR[o].astype(f32)
        sS[...] = tot.astype(bf16)
        sR[c] = tot.astype(bf16)
        cp = rc(b0 + 8, sS, sR.at[c], mate)
        cp.start()
        return cp

    def exchange_done(cp, fwd):
        tR, sR = tRs.at[0 if fwd else 1], sRs.at[0 if fwd else 1]
        cp.wait_recv()
        mate_base = (s + 1 - 2 * c) * LEN
        mate_open = flag(cnt(mate_base - 1) == cnt(mate_base + LEN - 1))
        second = (c == 1) if fwd else (c == 0)
        out = []
        for hd in range(2):
            far = sR[hd].astype(f32)
            out.append(jnp.where(second, tR[hd].astype(f32) + mate_open * far, far))
        return out

    def spread(dst, b, state):
        zero = jnp.zeros((HD, HD), bf16)
        dst[b] = jnp.concatenate([jnp.concatenate([state[0].astype(bf16), zero], axis=1),
                                  jnp.concatenate([zero, state[1].astype(bf16)], axis=1)], axis=0)

    lane = lax.broadcasted_iota(i32, (HD, HD), 1)

    def chunk(j):
        return pl.ds(pl.multiple_of(j * HD, HD), HD)

    def sums_start(S_ref, R_ref, b0):
        S_ref[...] = jnp.transpose(acc[...])[:16]
        cps = [rc(b0 + o - 1, S_ref, R_ref.at[o], head_peer(o)) for o in range(1, 16)]
        for one in cps:
            one.start()
        return cps

    def sums_finish(S_ref, R_ref, cps):
        tot = S_ref[...]
        for o in range(1, 16):
            cps[o - 1].wait_recv()
            tot = tot + R_ref[o]
        return jnp.transpose(jnp.concatenate([tot, jnp.zeros((HD - 16, HD), f32)], axis=0))

    def column(ref, j):
        return jnp.sum(jnp.where(lane == j, ref, 0.0), axis=1, keepdims=True)

    def tile_mask(b, r0, c0, ncol, rows_first):
        rr = pl.ds(pl.multiple_of(b * BLK + r0, 256), 256)
        cc = pl.ds(pl.multiple_of(b * BLK + c0, 256), ncol)
        rowc = jnp.concatenate([DC[rr, :]] * (ncol // HD), axis=1)
        same = rowc == DR[0:1, cc]
        ri = r0 + lax.broadcasted_iota(i32, (256, ncol), 0)
        ci = c0 + lax.broadcasted_iota(i32, (256, ncol), 1)
        return same & ((ci <= ri) if rows_first else (ri <= ci))

    def sub(ref, b, r0, nrow, hd):
        return ref[pl.ds(pl.multiple_of(b * BLK + r0, 256), nrow), hd * HD:(hd + 1) * HD]

    def forward(b):
        for ti in range(2):
            ns = 256 * (ti + 1)
            m = tile_mask(b, 256 * ti, 0, ns, True)
            for hd in range(2):
                sc = nt(sub(q, b, 256 * ti, 256, hd), sub(k, b, 0, ns, hd))
                pr = jnp.where(m, sc, 0.0).astype(bf16)
                attn[pl.ds(pl.multiple_of(b * BLK + 256 * ti, 256), 256), hd * HD:(hd + 1) * HD] = nn(pr, sub(v, b, 0, ns, hd))

    def backward(b):
        for si in range(2):
            t0 = 256 * si
            ntok = BLK - t0
            m = tile_mask(b, 256 * si, t0, ntok, False)
            out = pl.ds(pl.multiple_of(b * BLK + 256 * si, 256), 256)
            for hd in range(2):
                cols_ = slice(hd * HD, (hd + 1) * HD)
                gt = sub(g, b, t0, ntok, hd)
                qt = sub(q, b, t0, ntok, hd)
                pt = jnp.where(m, nt(sub(k, b, 256 * si, 256, hd), qt), 0.0).astype(bf16)
                GV[out, cols_] = nn(pt, gt)
                dt = jnp.where(m, nt(sub(v, b, 256 * si, 256, hd), gt), 0.0).astype(bf16)
                GK[out, cols_] = nn(dt, qt)
        for ti in range(2):
            ns = 256 * (ti + 1)
            m = tile_mask(b, 256 * ti, 0, ns, True)
            out = pl.ds(pl.multiple_of(b * BLK + 256 * ti, 256), 256)
            keep = wide(DC[out, :]) == edge_at(b)
            inter = jnp.where(keep, nt(g[out, :], F[b]), 0.0)
            for hd in range(2):
                cols_ = slice(hd * HD, (hd + 1) * HD)
                dp = jnp.where(m, nt(sub(g, b, 256 * ti, 256, hd), sub(v, b, 0, ns, hd)), 0.0).astype(bf16)
                gq_o[out, cols_] = (nn(dp, sub(k, b, 0, ns, hd)) + inter[:, cols_]).astype(bf16)

    def mix_store(p, r, val):
        if p == 0:
            GM[zh, x_of[r]] = val
        else:
            SG[p - 1, r] = val
            mix(p, r).start()

    def mix_rows(p, r, h0, h1):
        a = R[r].reshape(HD, D)
        return nt(a, W[p].reshape(WID, D)).astype(bf16)

    def w_here(p):
        wgt[p - 1].wait_recv()
        if p < 3:
            wgt[p].start()
        for cp in wys[p][:3]:
            cp.start()

    def w_relay(p):
        a = wys[p]
        a[0].wait_recv()
        a[3].start()
        a[5].start()
        a[1].wait_recv()
        a[4].start()
        a[6].start()

    def w_last(p):
        a = wys[p]
        a[3].wait_recv()
        a[4].wait_recv()
        a[7].start()

    def w_mate(p):
        a = wys[p]
        for i in (2, 5, 6, 7):
            a[i].wait_recv()

    local[0].wait()
    local[1].wait()
    lax.fori_loop(0, NB, functools.partial(elements, left_ref=k, right_ref=v, at_end=True), 0)
    x1 = exchange_send(FST0, range(NB))
    local[2].wait()
    forward(0)
    x2 = exchange_chip(FST0, x1, True)
    w_here(1)
    forward(1)
    x3 = exchange_mate(FST0, x2, True)
    forward(2)
    w_here(2)
    w_relay(1)
    forward(3)
    rows[0].wait_recv()
    rows[4].start()
    rows[2].wait_recv()
    rows[5].start()
    state = exchange_done(x3, True)
    for b in range(NB):
        spread(F, b, state)
        state = [E[b, hd] + open_[b] * state[hd] for hd in range(2)]
    w_here(3)
    w_last(1)

    def inter(b, _):
        r = rows_at(b)
        keep = wide(DC[r, :]) == edge_at(b)
        attn[r, :] = attn[r, :] + jnp.where(keep, nn(q[r, :], F[b]), 0.0)
        return 0

    lax.fori_loop(0, NB, inter, 0)
    acc[...] = jnp.zeros((HD, HD), f32)

    def squares(j, _):
        a = attn[chunk(j), :]
        acc[...] = jnp.where(lane == j, jnp.sum(a * a, axis=1, keepdims=True), acc[...])
        return 0

    lax.fori_loop(0, 16, squares, 0)
    x4 = sums_start(sqS, sqR, SQ0)
    w_relay(2)
    local[4].wait()
    local[5].wait()
    mix_store(0, 0, mix_rows(0, 0, 0, 2))
    w_mate(1)
    mix_store(1, 0, mix_rows(1, 0, 0, 2))
    w_last(2)
    w_relay(3)
    rows[1].wait_recv()
    for p in (0, 1):
        mix_store(p, 1, mix_rows(p, 1, 0, 2))
    rows[3].wait_recv()
    for p in (0, 1):
        mix_store(p, 2, mix_rows(p, 2, 0, 2))
    w_mate(2)
    for r in (0, 1, 2):
        mix_store(2, r, mix_rows(2, r, 0, 2))
    w_last(3)
    w_mate(3)
    for r in (0, 1, 2):
        mix_store(3, r, mix_rows(3, r, 0, 2))
    rows[4].wait_recv()
    rows[5].wait_recv()
    for p in (3, 1, 2, 0):
        mix_store(p, 3, mix_rows(p, 3, 0, 2))

    sq = sums_finish(sqS, sqR, x4)
    rms = jnp.sqrt(sq / HDIM + EPS)
    cols[0] = 1.0 / rms
    local[3].wait()
    for p in (1, 2, 3):
        for r in range(4):
            mix(p, r).wait_recv()

    acc[...] = jnp.zeros((HD, HD), f32)

    def gm_at(j):
        return GM[lax.div(j, 4), lax.rem(j, 4)].astype(f32)

    def cross(j, _):
        a = attn[chunk(j), :]
        m = gm_at(j)
        acc[...] = jnp.where(lane == j, jnp.sum(m * gate[chunk(j), :].astype(f32) * a, axis=1, keepdims=True), acc[...])
        return 0

    lax.fori_loop(0, 16, cross, 0)
    x5 = sums_start(crS, crR, CR0)

    def gate_grad(j, _):
        inv = column(cols[0], j)
        gg_o[chunk(j), :] = (gm_at(j) * attn[chunk(j), :] * inv).astype(bf16)
        return 0

    lax.fori_loop(0, 16, gate_grad, 0)
    cr = sums_finish(crS, crR, x5)
    inv = cols[0]
    cols[1] = cr * inv * inv * inv / HDIM

    def attn_grad(j, _):
        inv = column(cols[0], j)
        cc = column(cols[1], j)
        a = attn[chunk(j), :]
        g[chunk(j), :] = (gm_at(j) * gate[chunk(j), :].astype(f32) * inv - a * cc).astype(bf16)
        return 0

    lax.fori_loop(0, 16, attn_grad, 0)

    lax.fori_loop(0, NB, functools.partial(elements, left_ref=q, right_ref=g, at_end=False), 0)
    x6 = exchange_send(RST0, range(NB - 1, -1, -1))
    backward(0)
    x7 = exchange_chip(RST0, x6, False)
    backward(1)
    backward(2)
    x8 = exchange_mate(RST0, x7, False)
    backward(3)
    state = exchange_done(x8, False)
    for b in range(NB - 1, -1, -1):
        spread(PS, b, state)
        state = [E[b, hd] + open_[b] * state[hd] for hd in range(2)]

    def finish(b, _):
        r = rows_at(b)
        keep = wide(DC[r, :]) == edge_at(b + 1)
        gk_o[r, :] = (GK[r, :] + jnp.where(keep, nt(v[r, :], PS[b]), 0.0)).astype(bf16)
        gv_o[r, :] = (GV[r, :] + jnp.where(keep, nn(k[r, :], PS[b]), 0.0)).astype(bf16)
        return 0

    lax.fori_loop(0, NB, finish, 0)

    for cp in rows + wgt + wys[1] + wys[2] + wys[3] + [mix(p, r) for p in (1, 2, 3) for r in range(4)] + x4 + x5 + [x1] + x2 + [x3, x6] + x7 + [x8]:
        cp.wait_send()


def body(out_grad, out_weight, queries, key_rows, value_rows, gate_out, doc_starts):
    any_ = pl.BlockSpec(memory_space=pl.ANY)
    vm = pl.BlockSpec(memory_space=pltpu.VMEM)
    out = jax.ShapeDtypeStruct((LEN, WID), bf16)
    V = pltpu.VMEM
    return pl.pallas_call(
        kernel,
        out_shape=(out,) * 4,
        in_specs=[pl.BlockSpec(memory_space=pltpu.SMEM)] + [any_] * 6,
        out_specs=(vm,) * 4,
        scratch_shapes=[
            V((4, 2, 64, D), bf16),
            V((4, 2, 4, 32, D), bf16),
            V((LEN, WID), bf16), V((LEN, WID), bf16), V((LEN, WID), bf16), V((LEN, WID), bf16),
            V((LEN, WID), f32),
            V((4, 4, HD, WID), bf16),
            V((3, 4, HD, WID), bf16),
            V((LEN, WID), bf16),
            V((LEN, WID), f32), V((LEN, WID), f32),
            V((LEN, HD), i32), V((8, LEN), i32),
            V((NB, 2, HD, HD), f32),
            V((NB, WID, WID), bf16), V((NB, WID, WID), bf16),
            V((2, 2, HD, HD), bf16), V((2, 2, HD, HD), bf16),
            V((2, 2, HD, HD), bf16), V((2, 8, HD, HD), bf16),
            V((2, HD, HD), bf16), V((2, 2, HD, HD), bf16),
            V((2, HD, HD), f32),
            V((16, HD), f32), V((16, 16, HD), f32),
            V((16, HD), f32), V((16, 16, HD), f32),
            V((HD, HD), f32), V((2, HD, HD), f32),
            pltpu.SemaphoreType.DMA((NSEM,)), pltpu.SemaphoreType.DMA((NSEM,)), pltpu.SemaphoreType.DMA((6,)),
        ],
        compiler_params=pltpu.CompilerParams(collective_id=0, has_side_effects=True, vmem_limit_bytes=63000000),
        name="layer_backward",
    )(doc_starts, out_grad.reshape(2, 64, D), out_weight.reshape(2, 4, 32, D), queries, key_rows, value_rows, gate_out)


def solution(mesh):
    return jax.shard_map(
        body,
        mesh=mesh,
        in_specs=(P(("seq", "head"), None), P("head", None), P("seq", "head"), P("seq", "head"), P("seq", "head"),
                  P("seq", "head"), P()),
        out_specs=(P("seq", "head"),) * 4,
        check_vma=False,
    )
```

```python
import functools

import jax
import jax.numpy as jnp
from jax import lax
from jax.experimental import pallas as pl
from jax.experimental.pallas import tpu as pltpu
from jax.sharding import PartitionSpec as P

HD = 128
BLK = 512
HDIM = 4096
D = 4096
DOCS = 9
LEN = 2048
WID = 256
NB = 4
EPS = 1e-06
MESH = pl.DeviceIdType.MESH
f32 = jnp.float32
bf16 = jnp.bfloat16
i32 = jnp.int32

ROW0, WGT0, WY0, MIX0, FST0, RST0, SQ0, CR0, NSEM = 0, 12, 18, 42, 54, 63, 72, 78, 93


def nt(a, b):
    return lax.dot_general(a, b, (((1,), (1,)), ((), ())), preferred_element_type=f32)


def nn(a, b):
    return lax.dot_general(a, b, (((1,), (0,)), ((), ())), preferred_element_type=f32)


def tn(a, b):
    return lax.dot_general(a, b, (((0,), (0,)), ((), ())), preferred_element_type=f32)


def kernel(ds, og, w, q_h, k_h, v_h, gate_h, gq_o, gk_o, gv_o, gg_o,
           gqs, gks, gvs, ggs,
           R, W, q, k, v, gate, attn, GM, SG, g, GK, GV, DC, DR, E, F, PS,
           tSf, tRf, cSf, cRf, sSf, sRf, tSr, tRr, cSr, cRr, sSr, sRr, st, sqS, sqR, sq2S, sq2R, crS, crR, cols,
           ssem, rsem, lsem, osem):
    s = lax.axis_index("seq")
    h = lax.axis_index("head")
    c = lax.rem(s, 2)
    zl = lax.rem(lax.div(s, 2), 2)
    y = lax.div(s, 4)
    x = lax.rem(h, 4)
    zh = lax.div(h, 4)
    n = y * 2 + zl
    d = 2 * zl - 1

    def m4(a):
        return lax.rem(a + 8, 4)

    def dev(y_, zl_, c_, zh_, x_):
        return ((y_ * 2 + zl_) * 2 + c_, zh_ * 4 + x_)

    right = dev(y, zl, c, zh, m4(x + 1))
    left = dev(y, zl, c, zh, m4(x - 1))
    up = dev(m4(y + 1), zl, c, zh, x)
    down = dev(m4(y - 1), zl, c, zh, x)
    inner = dev(y, 1 - zl, c, zh, x)
    outer = dev(y, 1 - zl, c, m4(zh + d), x)
    mate = dev(y, zl, 1 - c, zh, x)
    zh_of = (zh, m4(zh + d), m4(zh - d), m4(zh + 2))
    x_of = (x, m4(x - 1), m4(x + 1), m4(x + 2))
    y_dn, y_up, y_op = m4(y - 1), m4(y + 1), m4(y + 2)

    def rc(i, src, dst, to):
        return pltpu.make_async_remote_copy(src_ref=src, dst_ref=dst, send_sem=ssem.at[i], recv_sem=rsem.at[i],
                                            device_id=to, device_id_type=MESH)

    def head_peer(o):
        return (s, lax.rem(h + o, 16))

    def chip_peer(o):
        m = lax.rem(n + o, 8)
        return (m * 2 + c, h)

    rows = [rc(i, og.at[i], R.at[1, i], right) for i in range(4)]
    rows += [rc(4 + i, og.at[i], R.at[2, i], left) for i in range(4)]
    rows += [rc(8 + i, R.at[1, i], R.at[3, i], right) for i in (0, 1)]
    rows += [rc(8 + i, R.at[2, i], R.at[3, i], left) for i in (2, 3)]
    halves = (pl.ds(0, 16), pl.ds(16, 16))
    own_w = [rc(WGT0 + i, w.at[c, y, hf], W.at[1, c, y, hf], outer) for i, hf in enumerate(halves)]
    near_w = [rc(WGT0 + 2 + i, W.at[1, c, y, hf], W.at[2, c, y, hf], inner) for i, hf in enumerate(halves)]
    far_w = [rc(WGT0 + 4 + i, W.at[2, c, y, hf], W.at[3, c, y, hf], outer) for i, hf in enumerate(halves)]
    top, bot = halves

    def wy(p):
        b = WY0 + 8 * (p - 1)
        return [
            rc(b, W.at[p, c, y], W.at[p, c, y], up),
            rc(b + 1, W.at[p, c, y], W.at[p, c, y], down),
            rc(b + 2, W.at[p, c, y], W.at[p, c, y], mate),
            rc(b + 3, W.at[p, c, y_dn, top], W.at[p, c, y_dn, top], up),
            rc(b + 4, W.at[p, c, y_up, bot], W.at[p, c, y_up, bot], down),
            rc(b + 5, W.at[p, c, y_dn], W.at[p, c, y_dn], mate),
            rc(b + 6, W.at[p, c, y_up], W.at[p, c, y_up], mate),
            rc(b + 7, W.at[p, c, y_op], W.at[p, c, y_op], mate),
        ]

    wys = {p: wy(p) for p in (1, 2, 3)}

    def mix(p, r):
        return rc(MIX0 + (p - 1) * 4 + r, SG.at[p - 1, r], GM.at[zh, x_of[r]], dev(y, zl, c, zh_of[p], x))

    local = [
        pltpu.make_async_copy(k_h, k, lsem.at[0]),
        pltpu.make_async_copy(v_h, v, lsem.at[1]),
        pltpu.make_async_copy(q_h, q, lsem.at[2]),
        pltpu.make_async_copy(gate_h, gate, lsem.at[3]),
        pltpu.make_async_copy(og, R.at[0], lsem.at[4]),
        pltpu.make_async_copy(w, W.at[0], lsem.at[5]),
    ]
    for cp in local[:3]:
        cp.start()

    barrier = pltpu.get_barrier_semaphore()
    for o in range(8):
        cRf[o] = jnp.zeros((HD, HD), f32)
        cRr[o] = jnp.zeros((HD, HD), bf16)
    peers = [chip_peer(o) for o in range(1, 8)] + [mate, outer, left, right, dev(y, zl, c, zh, m4(x + 2))]
    for to in peers:
        pl.semaphore_signal(barrier, inc=1, device_id=to, device_id_type=MESH)
    pl.semaphore_wait(barrier, len(peers))

    for cp in own_w:
        cp.start()
    for i in range(4):
        rows[i].start()
        rows[7 - i].start()
    for cp in local[3:]:
        cp.start()

    def cnt(t):
        total = jnp.int32(0)
        for i in range(DOCS):
            total = total + (ds[i] <= t).astype(i32)
        return total

    base = s * LEN
    edge = [cnt(base + BLK * b - 1) for b in range(NB + 1)]
    open_ = [(edge[b] == edge[b + 1]).astype(f32) for b in range(NB)]

    def edge_at(b):
        return cnt(base + BLK * b - 1)

    def rows_at(b):
        return pl.ds(pl.multiple_of(b * BLK, BLK), BLK)

    def counts(b, _):
        t = base + b * BLK + lax.broadcasted_iota(i32, (BLK, HD), 0)
        total = jnp.zeros((BLK, HD), i32)
        for i in range(DOCS):
            total = total + (t >= ds[i]).astype(i32)
        DC[rows_at(b), :] = total
        return 0

    lax.fori_loop(0, NB, counts, 0)
    t = base + lax.broadcasted_iota(i32, (8, LEN), 1)
    total = jnp.zeros((8, LEN), i32)
    for i in range(DOCS):
        total = total + (t >= ds[i]).astype(i32)
    DR[...] = total

    def wide(a):
        return jnp.concatenate([a, a], axis=1)

    def elements(b, _, left_ref, right_ref, at_end):
        r = rows_at(b)
        want = jnp.where(at_end, edge_at(b + 1), edge_at(b))
        keep = wide(DC[r, :]) == want
        a = jnp.where(keep, left_ref[r, :].astype(f32), 0.0).astype(bf16)
        both = tn(a, right_ref[r, :])
        E[b, 0] = both[:HD, :HD]
        E[b, 1] = both[HD:, HD:]
        return 0

    def flag(a):
        return jnp.where(a, 1.0, 0.0).astype(f32)

    mate_base = (s + 1 - 2 * c) * LEN
    mate_open = flag(cnt(mate_base - 1) == cnt(mate_base + LEN - 1))
    mine_open = flag(edge[0] == edge[NB])

    class Exchange:
        def __init__(self, b0, bufs, fwd):
            self.tS, self.tR, self.cS, self.cR, self.sS, self.sR = bufs
            self.fwd = fwd
            self.kind = self.tS.dtype
            self.second = (c == 1) if fwd else (c == 0)
            self.one = rc(b0, self.tS, self.tR, mate)
            self.chips = [rc(b0 + o, self.cS.at[c], self.cR.at[o], chip_peer(o)) for o in range(1, 8)]
            self.last = rc(b0 + 8, self.sS, self.sR.at[c], mate)

        def sends(self, o):
            return (n + o < 8) if self.fwd else (n + o >= 8)

        def gets(self, o):
            return (n - o >= 0) if self.fwd else (n - o < 0)

        def start(self):
            for hd in range(2):
                tot = jnp.zeros((HD, HD), f32)
                for b in (range(NB) if self.fwd else range(NB - 1, -1, -1)):
                    tot = E[b, hd] + open_[b] * tot
                st[hd] = tot
                self.tS[hd] = tot.astype(self.kind)
            self.one.start()

        def chip(self):
            self.one.wait_recv()
            mine_w = jnp.where(self.second, jnp.float32(1.0), mate_open)
            mate_w = jnp.where(self.second, mine_open, jnp.float32(1.0))
            for hd in range(2):
                self.cS[hd] = (mine_w * st[hd] + mate_w * self.tR[hd].astype(f32)).astype(self.kind)
            for o in range(1, 8):
                pl.when(self.sends(o))(self.chips[o - 1].start)

        def mate(self):
            for o in range(1, 8):
                pl.when(self.gets(o))(self.chips[o - 1].wait_recv)
            tot = jnp.zeros((HD, HD), f32)
            for o in range(1, 8):
                src = lax.rem(n - o + 8, 8)
                if self.fwd:
                    use = self.gets(o) & (cnt((src + 1) * 2 * LEN - 1) == cnt(n * 2 * LEN - 1))
                else:
                    use = self.gets(o) & (cnt((n + 1) * 2 * LEN - 1) == cnt(src * 2 * LEN - 1))
                tot = tot + flag(use) * self.cR[o].astype(f32)
            self.sS[...] = tot.astype(self.kind)
            self.sR[c] = tot.astype(self.kind)
            self.last.start()

        def done(self):
            self.last.wait_recv()
            out = []
            for hd in range(2):
                far = self.sR[hd].astype(f32)
                out.append(jnp.where(self.second, self.tR[hd].astype(f32) + mate_open * far, far))
            return out

        def drain(self):
            self.one.wait_send()
            for o in range(1, 8):
                pl.when(self.sends(o))(self.chips[o - 1].wait_send)
            self.last.wait_send()

    early = Exchange(FST0, (tSf, tRf, cSf, cRf, sSf, sRf), True)
    late = Exchange(RST0, (tSr, tRr, cSr, cRr, sSr, sRr), False)

    def spread(dst, b, state):
        zero = jnp.zeros((HD, HD), bf16)
        dst[b] = jnp.concatenate([jnp.concatenate([state[0].astype(bf16), zero], axis=1),
                                  jnp.concatenate([zero, state[1].astype(bf16)], axis=1)], axis=0)

    lane = lax.broadcasted_iota(i32, (HD, HD), 1)

    def chunk(j):
        return pl.ds(pl.multiple_of(j * HD, HD), HD)

    def columns_of(tot):
        return jnp.transpose(jnp.concatenate([tot, jnp.zeros((HD - 16, HD), f32)], axis=0))

    def column(ref, j):
        return jnp.sum(jnp.where(lane == j, ref, 0.0), axis=1, keepdims=True)

    def tile_mask(b, r0, c0, ncol, rows_first):
        rr = pl.ds(pl.multiple_of(b * BLK + r0, 256), 256)
        cc = pl.ds(pl.multiple_of(b * BLK + c0, 256), ncol)
        rowc = jnp.concatenate([DC[rr, :]] * (ncol // HD), axis=1)
        same = rowc == DR[0:1, cc]
        ri = r0 + lax.broadcasted_iota(i32, (256, ncol), 0)
        ci = c0 + lax.broadcasted_iota(i32, (256, ncol), 1)
        return same & ((ci <= ri) if rows_first else (ri <= ci))

    def sub(ref, b, r0, nrow, hd):
        return ref[pl.ds(pl.multiple_of(b * BLK + r0, 256), nrow), hd * HD:(hd + 1) * HD]

    def forward(b):
        for ti in range(2):
            ns = 256 * (ti + 1)
            m = tile_mask(b, 256 * ti, 0, ns, True)
            for hd in range(2):
                sc = nt(sub(q, b, 256 * ti, 256, hd), sub(k, b, 0, ns, hd))
                pr = jnp.where(m, sc, 0.0).astype(bf16)
                attn[pl.ds(pl.multiple_of(b * BLK + 256 * ti, 256), 256), hd * HD:(hd + 1) * HD] = nn(pr, sub(v, b, 0, ns, hd))

    def backward(b):
        for si in range(2):
            t0 = 256 * si
            ntok = BLK - t0
            m = tile_mask(b, 256 * si, t0, ntok, False)
            out = pl.ds(pl.multiple_of(b * BLK + 256 * si, 256), 256)
            for hd in range(2):
                cols_ = slice(hd * HD, (hd + 1) * HD)
                gt = sub(g, b, t0, ntok, hd)
                qt = sub(q, b, t0, ntok, hd)
                pt = jnp.where(m, nt(sub(k, b, 256 * si, 256, hd), qt), 0.0).astype(bf16)
                GV[out, cols_] = nn(pt, gt)
                dt = jnp.where(m, nt(sub(v, b, 256 * si, 256, hd), gt), 0.0).astype(bf16)
                GK[out, cols_] = nn(dt, qt)
        for ti in range(2):
            ns = 256 * (ti + 1)
            m = tile_mask(b, 256 * ti, 0, ns, True)
            out = pl.ds(pl.multiple_of(b * BLK + 256 * ti, 256), 256)
            keep = wide(DC[out, :]) == edge_at(b)
            inter = jnp.where(keep, nt(g[out, :], F[b]), 0.0)
            for hd in range(2):
                cols_ = slice(hd * HD, (hd + 1) * HD)
                dp = jnp.where(m, nt(sub(g, b, 256 * ti, 256, hd), sub(v, b, 0, ns, hd)), 0.0).astype(bf16)
                gqs[out, cols_] = (nn(dp, sub(k, b, 0, ns, hd)) + inter[:, cols_]).astype(bf16)

    def mix_rows(p, rs):
        a = R[rs[0]:rs[-1] + 1].reshape(len(rs) * HD, D)
        val = nt(a, W[p].reshape(WID, D)).astype(bf16)
        for i, r in enumerate(rs):
            part = val[i * HD:(i + 1) * HD]
            if p == 0:
                GM[zh, x_of[r]] = part
            else:
                SG[p - 1, r] = part
                mix(p, r).start()

    def w_relay(p):
        a = wys[p]
        a[0].wait_recv()
        a[3].start()
        a[5].start()
        a[1].wait_recv()
        a[4].start()
        a[6].start()

    def w_last(p):
        a = wys[p]
        a[3].wait_recv()
        a[4].wait_recv()
        a[7].start()

    def w_mate(p):
        a = wys[p]
        for i in (2, 5, 6, 7):
            a[i].wait_recv()

    def w_out(p):
        for cp in wys[p][:3]:
            cp.start()

    local[0].wait()
    local[1].wait()
    lax.fori_loop(0, NB, functools.partial(elements, left_ref=k, right_ref=v, at_end=True), 0)
    early.start()
    local[2].wait()
    forward(0)
    own_w[0].wait_recv()
    near_w[0].start()
    early.chip()
    forward(1)
    own_w[1].wait_recv()
    near_w[1].start()
    w_out(1)
    near_w[0].wait_recv()
    far_w[0].start()
    forward(2)
    early.mate()
    near_w[1].wait_recv()
    far_w[1].start()
    forward(3)
    state = early.done()
    for b in range(NB):
        spread(F, b, state)
        state = [E[b, hd] + open_[b] * state[hd] for hd in range(2)]

    def inter(b, _):
        r = rows_at(b)
        keep = wide(DC[r, :]) == edge_at(b)
        attn[r, :] = attn[r, :] + jnp.where(keep, nn(q[r, :], F[b]), 0.0)
        return 0

    lax.fori_loop(0, NB, inter, 0)
    w_relay(1)
    far_w[0].wait_recv()
    far_w[1].wait_recv()
    w_out(3)
    w_out(2)

    def squares(j, acc):
        a = attn[chunk(j), :]
        return jnp.where(lane == j, jnp.sum(a * a, axis=1, keepdims=True), acc)

    sqS[...] = jnp.transpose(lax.fori_loop(0, 16, squares, jnp.zeros((HD, HD), f32), unroll=2))[:16]
    x4 = [rc(SQ0 + o - 1, sqS, sqR.at[o], dev(y, zl, c, zh, m4(x + o))) for o in range(1, 4)]
    x4b = [rc(SQ0 + 2 + o, sq2S, sq2R.at[o], dev(y, zl, c, m4(zh + o), x)) for o in range(1, 4)]
    for cp in x4:
        cp.start()
    for i, j in ((0, 8), (7, 11), (1, 9), (6, 10)):
        rows[i].wait_recv()
        rows[j].start()
    local[4].wait()
    local[5].wait()
    mix_rows(0, (0,))
    tot = sqS[...]
    for o in range(1, 4):
        x4[o - 1].wait_recv()
        tot = tot + sqR[o]
    sq2S[...] = tot
    for cp in x4b:
        cp.start()
    w_last(1)
    w_mate(1)
    mix_rows(1, (0,))
    w_relay(3)
    for i in (2, 3, 5, 4):
        rows[i].wait_recv()
    mix_rows(1, (1, 2))
    mix_rows(0, (1, 2))
    w_relay(2)
    w_last(3)
    w_mate(3)
    mix_rows(3, (0, 1, 2))
    for o in range(1, 4):
        x4b[o - 1].wait_recv()
    tot = sq2S[...]
    for o in range(1, 4):
        tot = tot + sq2R[o]
    cols[0] = columns_of(1.0 / jnp.sqrt(tot / HDIM + EPS))
    local[3].wait()
    w_last(2)
    for i in (8, 11, 9, 10):
        rows[i].wait_recv()
    mix_rows(3, (3,))
    w_mate(2)
    mix_rows(2, (0, 1, 2, 3))
    mix_rows(1, (3,))
    mix_rows(0, (3,))

    for p in (1, 3, 2):
        for r in range(4):
            mix(p, r).wait_recv()

    def gm_at(j):
        return GM[lax.div(j, 4), lax.rem(j, 4)].astype(f32)

    def cross(j, acc):
        a = attn[chunk(j), :]
        m = gm_at(j)
        return jnp.where(lane == j, jnp.sum(m * gate[chunk(j), :].astype(f32) * a, axis=1, keepdims=True), acc)

    crS[...] = jnp.transpose(lax.fori_loop(0, 16, cross, jnp.zeros((HD, HD), f32), unroll=4))[:16]
    x5 = [rc(CR0 + o - 1, crS, crR.at[o], head_peer(o)) for o in range(1, 16)]
    for cp in x5:
        cp.start()

    def gate_grad(j, _):
        inv = column(cols[0], j)
        ggs[chunk(j), :] = (gm_at(j) * attn[chunk(j), :] * inv).astype(bf16)
        return 0

    lax.fori_loop(0, 16, gate_grad, 0, unroll=4)
    outs = [pltpu.make_async_copy(ggs, gg_o, osem.at[0])]
    outs[0].start()
    tot = crS[...]
    for o in range(1, 16):
        x5[o - 1].wait_recv()
        tot = tot + crR[o]
    inv = cols[0]
    cols[1] = columns_of(tot) * inv * inv * inv / HDIM

    def attn_grad(j, _):
        inv = column(cols[0], j)
        cc = column(cols[1], j)
        a = attn[chunk(j), :]
        g[chunk(j), :] = (gm_at(j) * gate[chunk(j), :].astype(f32) * inv - a * cc).astype(bf16)
        return 0

    lax.fori_loop(0, 16, attn_grad, 0, unroll=4)

    lax.fori_loop(0, NB, functools.partial(elements, left_ref=q, right_ref=g, at_end=False), 0, unroll=True)
    late.start()
    backward(0)
    late.chip()
    backward(1)
    backward(2)
    late.mate()
    backward(3)
    outs.append(pltpu.make_async_copy(gqs, gq_o, osem.at[1]))
    outs[1].start()
    state = late.done()
    for b in range(NB - 1, -1, -1):
        spread(PS, b, state)
        state = [E[b, hd] + open_[b] * state[hd] for hd in range(2)]

    for b in range(NB):
        r = pl.ds(b * BLK, BLK)
        keep = wide(DC[r, :]) == edge[b + 1]
        gks[r, :] = (GK[r, :] + jnp.where(keep, nt(v[r, :], PS[b]), 0.0)).astype(bf16)
        gvs[r, :] = (GV[r, :] + jnp.where(keep, nn(k[r, :], PS[b]), 0.0)).astype(bf16)
        two = [pltpu.make_async_copy(gks.at[r], gk_o.at[r], osem.at[2 + b]),
               pltpu.make_async_copy(gvs.at[r], gv_o.at[r], osem.at[6 + b])]
        for cp in two:
            cp.start()
        outs += two

    for cp in rows + own_w + near_w + far_w + wys[1] + wys[2] + wys[3] + [mix(p, r) for p in (1, 2, 3) for r in range(4)] + x4 + x4b + x5:
        cp.wait_send()
    early.drain()
    late.drain()
    for cp in outs:
        cp.wait()


def body(out_grad, out_weight, queries, key_rows, value_rows, gate_out, doc_starts):
    any_ = pl.BlockSpec(memory_space=pl.ANY)
    out = jax.ShapeDtypeStruct((LEN, WID), bf16)
    V = pltpu.VMEM
    return pl.pallas_call(
        kernel,
        out_shape=(out,) * 4,
        in_specs=[pl.BlockSpec(memory_space=pltpu.SMEM)] + [any_] * 6,
        out_specs=(any_,) * 4,
        scratch_shapes=[V((LEN, WID), bf16)] * 4 + [
            V((4, 4, 32, D), bf16),
            V((4, 2, 4, 32, D), bf16),
            V((LEN, WID), bf16), V((LEN, WID), bf16), V((LEN, WID), bf16), V((LEN, WID), bf16),
            V((LEN, WID), f32),
            V((4, 4, HD, WID), bf16),
            V((3, 4, HD, WID), bf16),
            V((LEN, WID), bf16),
            V((LEN, WID), f32), V((LEN, WID), f32),
            V((LEN, HD), i32), V((8, LEN), i32),
            V((NB, 2, HD, HD), f32),
            V((NB, WID, WID), bf16), V((NB, WID, WID), bf16),
            V((2, HD, HD), f32), V((2, HD, HD), f32), V((2, HD, HD), f32), V((8, HD, HD), f32),
            V((HD, HD), f32), V((2, HD, HD), f32),
            V((2, HD, HD), bf16), V((2, HD, HD), bf16), V((2, HD, HD), bf16), V((8, HD, HD), bf16),
            V((HD, HD), bf16), V((2, HD, HD), bf16),
            V((2, HD, HD), f32),
            V((16, HD), f32), V((4, 16, HD), f32), V((16, HD), f32), V((4, 16, HD), f32),
            V((16, HD), f32), V((16, 16, HD), f32),
            V((2, HD, HD), f32),
            pltpu.SemaphoreType.DMA((NSEM,)), pltpu.SemaphoreType.DMA((NSEM,)), pltpu.SemaphoreType.DMA((6,)), pltpu.SemaphoreType.DMA((10,)),
        ],
        compiler_params=pltpu.CompilerParams(collective_id=0, has_side_effects=True, vmem_limit_bytes=63000000),
        name="layer_backward",
    )(doc_starts, out_grad.reshape(4, 32, D), out_weight.reshape(2, 4, 32, D), queries, key_rows, value_rows, gate_out)


def solution(mesh):
    return jax.shard_map(
        body,
        mesh=mesh,
        in_specs=(P(("seq", "head"), None), P("head", None), P("seq", "head"), P("seq", "head"), P("seq", "head"),
                  P("seq", "head"), P()),
        out_specs=(P("seq", "head"),) * 4,
        check_vma=False,
    )
```
